128 devices in a mesh: pair: 8 (over x, core), ints: 16 (over y, z).
Axes of the slice: x: 4, y: 4, z: 4, core: 2. Of those that a mesh axis runs over, the one named last changes fastest.
Arguments:
- t2: bfloat16 [4096, 8192], P('pair', 'ints'), may hold values from -6 to 6
- t2_live: int32 [8, 64], P('pair', 'ints'), may hold values 0 or 1
- int_tiles: int32 [5120, 2], P('ints'), may hold values from 0 to 63
- integrals: bfloat16 [5120, 128, 128], P('ints'), may hold values from -0.0625 to 0.0625
- cycle_w: bfloat16 [4096, 4096], P('pair'), may hold values from -0.09375 to 0.09375
- res_live: int32 [8, 64], P('pair', 'ints'), may hold values 0 or 1
Outputs:
- residual: float32 [4096, 8192], P('pair', 'ints')
The draws below stay inside these ranges and needn't reach their ends.
All inputs are finite; a program needn't handle non-finite values. No bound on the sum of `t2_live` or of `res_live` on one device may be relied on, other than what follows from the above.
Results may differ from the reference program's by a relative error of at most 0.0003.
Values may be sent and summed in bfloat16 or wider, within the bound.
No kernel may reach another device: no remote copies, remote signals or barrier semaphores. Data moves between devices by JAX's collectives and lax.ppermute only.
A program may use at most 192 MiB of HBM per device.

```python
import jax
import jax.numpy as jnp
from jax import lax

TILE = 128
NT_DEV = 4
VI_DEV = 320
NBLK = 8
PAIRS = 4096
NT = 64
NV = 5120


def touch_ends(values, own_key, least, high):
    place = [jax.random.randint(jax.random.fold_in(own_key, axis), (), 0, length) for axis, length in enumerate(values.shape)]
    main_axis = values.shape.index(max(values.shape))
    neighbour = place[:main_axis] + [(place[main_axis] + 1) % values.shape[main_axis]] + place[main_axis + 1:]
    return values.at[tuple(place)].set(least).at[tuple(neighbour)].set(high)


def levels(own_key, extent, pieces, smallest, top_value):
    factor_of = 1.0
    for axis_at, blocks in pieces:
        draws = jax.random.uniform(jax.random.fold_in(jax.random.fold_in(own_key, 6), axis_at), (blocks,), jnp.float32, smallest / len(pieces), top_value / len(pieces))
        factor_of = factor_of * jnp.repeat(jnp.exp(draws), extent[axis_at] // blocks).reshape((-1,) + (1,) * (len(extent) - 1 - axis_at))
    return factor_of


def noise(stream_key, extent, scale, bound, cuts=(), kind=jnp.bfloat16):
    array = jax.random.normal(stream_key, extent, jnp.float32) * scale
    if len(cuts) > 0:
        array = levels(stream_key, extent, cuts, -0.22, 0.18) * array
    return jnp.clip(array, min=-bound, max=bound).astype(kind)


def setup_inputs(seed: int = 0) -> dict:
    key_list = jax.random.split(jax.random.key(seed), 7)
    t2 = noise(key_list[0], (PAIRS, NT * TILE), 1.0, 6.0, ((0, 8), (1, 16)))
    t2_live = touch_ends((jax.random.randint(key_list[1], (NBLK, NT), 0, 4) < 3).astype(jnp.int32), jax.random.fold_in(key_list[1], 1), 0, 1)
    int_tiles = touch_ends(jax.random.randint(key_list[2], (NV, 2), 0, NT), jax.random.fold_in(key_list[2], 1), 0, NT - 1).astype(jnp.int32)
    integrals = noise(key_list[3], (NV, TILE, TILE), (TILE * VI_DEV // NT_DEV) ** -0.5, 0.0625, ((0, 16),))
    cycle_w = noise(key_list[4], (PAIRS, PAIRS), PAIRS ** -0.5, 0.09375, ((0, 8),))
    res_live = touch_ends((jax.random.randint(key_list[5], (NBLK, NT), 0, 4) < 3).astype(jnp.int32), jax.random.fold_in(key_list[5], 1), 0, 1)
    return {"t2": t2, "t2_live": t2_live, "int_tiles": int_tiles, "integrals": integrals, "cycle_w": cycle_w, "res_live": res_live}


def reference(t2, t2_live, int_tiles, integrals, cycle_w, res_live):
    pair_count = t2.shape[0]
    block_rows = pair_count // t2_live.shape[0]
    live_rows = jnp.repeat(t2_live, block_rows, axis=0).astype(t2.dtype)
    amps_tiled = t2.reshape(pair_count, NT, TILE) * live_rows[:, :, None]
    group_size = 64 if VI_DEV % 64 == 0 else VI_DEV
    all_tiles = int_tiles.reshape(NV // group_size, group_size, 2)
    all_ints = integrals.reshape(NV // group_size, group_size, TILE, TILE)

    def ladder_step(partial_value, entry):
        pairs_uv, blocks = entry
        picked = jnp.take(amps_tiled, pairs_uv[:, 0].astype(jnp.int32), axis=1)
        product = jnp.einsum("pjc,jcd->jpd", picked.astype(jnp.float32), blocks.astype(jnp.float32))
        partial_value = partial_value.at[pairs_uv[:, 1].astype(jnp.int32)].add(product)
        return partial_value, None

    total_start = jnp.zeros((NT, pair_count, TILE), jnp.float32)
    total, _ = lax.scan(ladder_step, total_start, (all_tiles, all_ints))
    ladder = total.transpose(1, 0, 2).reshape(pair_count, NT * TILE)
    cycle_term = jnp.dot(cycle_w, amps_tiled.reshape(pair_count, NT * TILE), preferred_element_type=jnp.float32)
    keep_rows = jnp.repeat(res_live, block_rows, axis=0)
    keep_mask = jnp.repeat(keep_rows, TILE, axis=1).astype(jnp.float32)
    return keep_mask * (ladder + cycle_term)
```

```python
import jax
import jax.numpy as jnp
import numpy as np
from jax import lax
from jax.experimental import pallas as pl
from jax.experimental.pallas import tpu as pltpu
from jax.sharding import PartitionSpec as P

ROWS = 512
TILE = 128
TILES = 64
SIDE = 4
PAD = 16
ENTRIES = 224
UNROLL = 8
HALF_RANGE = 14.9
VMEM_LIMIT = 58 * 1024 * 1024
NEAR = {0: 0, 1: 1, 3: 2, 2: 3}

VMEM_SPEC = pl.BlockSpec(memory_space=pltpu.VMEM)
SMEM_SPEC = pl.BlockSpec(memory_space=pltpu.SMEM)


def source_table():
    table = np.zeros((SIDE, SIDE, 4), np.int32)
    for dy in range(SIDE):
        for dz in range(SIDE):
            for t in range(2):
                table[dy, dz, t] = NEAR[dy] * 8 + NEAR[dz] * 2 + t
                table[dy, dz, t + 2] = 32 + NEAR[dz] * 8 + NEAR[dy] * 2 + t
    return table.reshape(-1)


def target_table():
    table = np.zeros((SIDE, SIDE, 4), np.int32)
    for far in range(SIDE):
        for other in range(SIDE):
            for t in range(2):
                if far == 2:
                    place = 0 if t == 0 else 8
                elif far == 1:
                    place = 32 if t == 0 else 4
                elif far == 3:
                    place = 12 if t == 0 else 36
                else:
                    place = 40 if t == 0 else 44
                sent = place < 16
                table[other, far, t] = place + other
                table[far, other, t + 2] = place + other + 16
    return table.reshape(-1)


def pick(table, index):
    spread = jnp.arange(TILES, dtype=jnp.int32)
    return jnp.sum(jnp.where(index[:, None] == spread[None, :], jnp.asarray(table)[None, :], 0), axis=1)


def relative(tile, y, z):
    device = tile >> 2
    dy = ((device >> 2) - y) & 3
    dz = ((device & 3) - z) & 3
    return (dy * SIDE + dz) * 4 + (tile & 3)


def work_list(source, target):
    count = source.shape[0]
    order = jnp.arange(count, dtype=jnp.int32)
    ids = jnp.arange(TILES, dtype=jnp.int32)
    same = target[:, None] == ids[None, :]
    held = jnp.sum(same, axis=0, dtype=jnp.int32)
    before = jnp.sum((target[None, :] == target[:, None]) & (order[None, :] < order[:, None]), axis=1, dtype=jnp.int32)
    entries = jnp.maximum((held + 1) // 2, 1)
    start = jnp.sum(jnp.where(ids[None, :] < ids[:, None], entries[None, :], 0), axis=1)
    mine = jnp.sum(jnp.where(same, start[None, :], 0), axis=1)
    slot = (mine + before // 2) * 2 + before % 2
    value = source + (order << 6) + (1 << 15)
    slots = jnp.arange(2 * ENTRIES, dtype=jnp.int32)
    tiles = jnp.sum(jnp.where(slot[:, None] == slots[None, :], value[:, None], 0), axis=0)
    at = jnp.arange(ENTRIES, dtype=jnp.int32)
    owner = jnp.sum(start[None, :] <= at[:, None], axis=1, dtype=jnp.int32) - 1
    fresh = jnp.sum(start[None, :] == at[:, None], axis=1, dtype=jnp.int32)
    bounds = jnp.concatenate([start, jnp.sum(entries)[None]])
    return tiles, owner * 2 + fresh, bounds


def encode(value):
    top = jnp.max(jnp.abs(value), axis=0, keepdims=True)
    power = jnp.floor(jnp.log2(jnp.maximum(top, 2.0**-100))) + 1.0
    whole = jnp.round(value * jnp.exp2(HALF_RANGE - power)).astype(jnp.int32).astype(jnp.int16)
    return whole, jnp.broadcast_to(power, (PAD, TILE)).astype(jnp.int32).astype(jnp.int16)


def put(ref, k, value):
    whole, power = encode(value)
    ref[k, 0:ROWS, :] = whole
    ref[k, ROWS : ROWS + PAD, :] = power


def get(ref, k):
    power = ref[k, ROWS : ROWS + PAD, :].astype(jnp.int32).astype(jnp.float32)[0:1, :]
    return ref[k, 0:ROWS, :].astype(jnp.int32).astype(jnp.float32) * jnp.exp2(power - HALF_RANGE)


def coded(n):
    return jax.ShapeDtypeStruct((n, ROWS + PAD, TILE), jnp.int16)


def plain(n):
    return jax.ShapeDtypeStruct((n, ROWS, TILE), jnp.float32)


def kernel(body, outs, specs, scratch=(), name=None):
    return pl.pallas_call(
        body,
        out_shape=outs,
        in_specs=specs,
        out_specs=jax.tree.map(lambda _: VMEM_SPEC, outs),
        scratch_shapes=list(scratch),
        compiler_params=pltpu.CompilerParams(vmem_limit_bytes=VMEM_LIMIT),
        name=name,
    )


def ladder(tiles, owner, bounds, amps, integrals, first, count, send):
    def body(tiles_ref, owner_ref, bounds_ref, amps_ref, ints_ref, *rest):
        sums = rest[-1] if send else rest[0]
        begin = bounds_ref[first]
        end = bounds_ref[first + count]

        def step(i, carry):
            for k in range(UNROLL):
                at = begin + i * UNROLL + k
                inside = at < end
                at = jnp.minimum(at, ENTRIES - 1)
                left = tiles_ref[2 * at]
                right = tiles_ref[2 * at + 1]
                mark = owner_ref[at]
                place = jnp.where(inside, (mark >> 1) - first, count - 1)
                fresh = jnp.logical_and(inside, (mark & 1) == 1)
                keep_left = jnp.where(inside, left >> 15, 0).astype(jnp.float32).astype(jnp.bfloat16)
                keep_right = jnp.where(inside, right >> 15, 0).astype(jnp.float32).astype(jnp.bfloat16)
                weights = jnp.concatenate(
                    [ints_ref[(left >> 6) & 511] * keep_left, ints_ref[(right >> 6) & 511] * keep_right], axis=0
                )
                values = jnp.concatenate([amps_ref[left & 63], amps_ref[right & 63]], axis=1)
                product = jnp.dot(values, weights, preferred_element_type=jnp.float32)
                sums[place] = product + jnp.where(fresh, 0.0, sums[place])
            return carry

        lax.fori_loop(0, (end - begin + UNROLL - 1) // UNROLL, step, 0)
        if send:
            half = count // 2

            def code(k, carry):
                put(rest[0], k, sums[k])
                put(rest[1], k, sums[k + half])
                return carry

            lax.fori_loop(0, half, code, 0)

    outs = (coded(count // 2), coded(count // 2)) if send else (plain(count),)
    scratch = [pltpu.VMEM((count, ROWS, TILE), jnp.float32)] if send else []
    specs = [SMEM_SPEC] * 3 + [VMEM_SPEC] * 2
    return kernel(body, outs, specs, scratch)(tiles, owner, bounds, amps, integrals)


def merge(sums, got_up, got_down, base):
    def body(sums_ref, up_ref, down_ref, up_out, down_out):
        def step(k, carry):
            put(up_out, k, sums_ref[base + k] + get(up_ref, k))
            put(down_out, k, sums_ref[base + 4 + k] + get(down_ref, k))
            return carry

        lax.fori_loop(0, 4, step, 0)

    return kernel(body, (coded(4), coded(4)), [VMEM_SPEC] * 3)(sums, got_up, got_down)


def row_sum(sums, got_up, got_down, last_up, last_down, base):
    def body(sums_ref, up_ref, down_ref, last_up_ref, last_down_ref, up_out, down_out, kept):
        def low(k):
            return sums_ref[base + 8 + k] + get(down_ref, 4 + k) + get(last_up_ref, k)

        def high(k):
            return sums_ref[base + 12 + k] + get(up_ref, 4 + k) + get(last_down_ref, k)

        put(up_out, 0, low(2))
        put(up_out, 1, high(1))
        put(down_out, 0, high(2))
        put(down_out, 1, low(3))
        kept[0] = low(1)
        kept[1] = high(3)
        kept[2] = low(0)
        kept[3] = high(0)

    return kernel(body, (coded(2), coded(2), plain(4)), [VMEM_SPEC] * 5)(sums, got_up, got_down, last_up, last_down)


def merge_last(kept, got_up, got_down):
    def body(kept_ref, up_ref, down_ref, up_out, down_out):
        put(up_out, 0, kept_ref[0] + get(up_ref, 0))
        put(down_out, 0, kept_ref[1] + get(down_ref, 0))

    return kernel(body, (coded(1), coded(1)), [VMEM_SPEC] * 3)(kept, got_up, got_down)


def finish(res_live, cycle, half_a, half_b):
    def body(live_ref, cycle_ref, *refs):
        out_ref = refs[-1]
        for h in range(2):
            kept, up, down, last_up, last_down = refs[5 * h : 5 * h + 5]
            low = kept[2] + get(down, 1) + get(last_up, 0)
            high = kept[3] + get(up, 1) + get(last_down, 0)
            for t, value in ((2 * h, low), (2 * h + 1, high)):
                cols = slice(t * TILE, (t + 1) * TILE)
                keep = live_ref[0, t].astype(jnp.float32)
                out_ref[:, cols] = keep * (value + cycle_ref[:, cols])

    out = jax.ShapeDtypeStruct((ROWS, 4 * TILE), jnp.float32)
    return kernel(body, out, [SMEM_SPEC] + [VMEM_SPEC] * 11)(res_live, cycle, *half_a, *half_b)


def local(t2, t2_live, int_tiles, integrals, cycle_w, res_live):
    place = lax.axis_index("ints").astype(jnp.int32)
    y, z = place >> 2, place & 3

    def take(value, dy, dz):
        pairs = [
            (((i + dy) % SIDE) * SIDE + (k + dz) % SIDE, i * SIDE + k) for i in range(SIDE) for k in range(SIDE)
        ]
        return lax.ppermute(value, "ints", pairs)

    def along_z(value, d):
        return take(value, 0, d)

    def along_y(value, d):
        return take(value, d, 0)

    mask = jnp.repeat(t2_live[0].astype(t2.dtype), TILE)
    flat = t2 * mask[None, :]
    own = flat.reshape(ROWS, 4, TILE).transpose(1, 0, 2)

    def gather(value, near_axis, far_axis):
        n = value.shape[0] // 2
        up, down = near_axis(value, 1), near_axis(value, 3)
        over = near_axis(up[:n], 1), near_axis(down[n:], 3)
        row = jnp.concatenate([value, up, down, *over], axis=0)
        n = row.shape[0] // 2
        up, down = far_axis(row, 1), far_axis(row, 3)
        over = far_axis(up[:n], 1), far_axis(down[n:], 3)
        return [row, up, down, *over]

    pieces_a = gather(own[:2], along_z, along_y)
    pieces_b = gather(own[2:], along_y, along_z)
    amps = jnp.concatenate(pieces_a + pieces_b, axis=0)

    source = pick(source_table(), relative(int_tiles[:, 0], y, z))
    target = pick(target_table(), relative(int_tiles[:, 1], y, z))
    tiles, owner, bounds = work_list(source, target)

    send_a = ladder(tiles, owner, bounds, amps, integrals, 0, 16, True)
    send_b = ladder(tiles, owner, bounds, amps, integrals, 16, 16, True)

    def first_hop(send, axis):
        return axis(send[0], 3), axis(send[1], 1)

    got_a = first_hop(send_a, along_z)
    got_b = first_hop(send_b, along_y)
    (sums,) = ladder(tiles, owner, bounds, amps, integrals, 32, 32, False)

    cycle = jnp.dot(
        cycle_w, lax.all_gather(flat, "pair", axis=0, tiled=True), preferred_element_type=jnp.float32
    )

    def reduce(got, axis, other, base):
        on = merge(sums, *got, base)
        last = first_hop(on, axis)
        up, down, kept = row_sum(sums, *got, *last, base)
        got = first_hop((up, down), other)
        last = first_hop(merge_last(kept, *got), other)
        return (kept, *got, *last)

    half_a = reduce(got_a, along_z, along_y, 0)
    half_b = reduce(got_b, along_y, along_z, 16)
    return finish(res_live, cycle, half_a, half_b)


def solution(mesh):
    placed = (
        P("pair", "ints"),
        P("pair", "ints"),
        P("ints", None),
        P("ints", None, None),
        P("pair", None),
        P("pair", "ints"),
    )
    return jax.shard_map(local, mesh=mesh, in_specs=placed, out_specs=P("pair", "ints"), check_vma=False)
```

```python
import jax
import jax.numpy as jnp
import numpy as np
from jax import lax
from jax.experimental import pallas as pl
from jax.experimental.pallas import tpu as pltpu
from jax.sharding import PartitionSpec as P

ROWS = 512
TILE = 128
TILES = 64
SIDE = 4
PAD = 16
ENTRIES = 224
UNROLL = 8
HALF_RANGE = 14.9
NEAR = {0: 0, 1: 1, 3: 2, 2: 3}

VMEM_SPEC = pl.BlockSpec(memory_space=pltpu.VMEM)
SMEM_SPEC = pl.BlockSpec(memory_space=pltpu.SMEM)


def source_table():
    table = np.zeros((SIDE, SIDE, 4), np.int32)
    for dy in range(SIDE):
        for dz in range(SIDE):
            for t in range(2):
                table[dy, dz, t] = NEAR[dy] * 8 + NEAR[dz] * 2 + t
                table[dy, dz, t + 2] = 32 + NEAR[dz] * 8 + NEAR[dy] * 2 + t
    return table.reshape(-1)


def target_table():
    table = np.zeros((SIDE, SIDE, 4), np.int32)
    for far in range(SIDE):
        for other in range(SIDE):
            for t in range(2):
                if far == 2:
                    place = 0 if t == 0 else 8
                elif far == 1:
                    place = 32 if t == 0 else 4
                elif far == 3:
                    place = 12 if t == 0 else 36
                else:
                    place = 40 if t == 0 else 44
                sent = place < 16
                table[other, far, t] = place + other
                table[far, other, t + 2] = place + other + 16
    return table.reshape(-1)


def pick(table, index):
    spread = jnp.arange(TILES, dtype=jnp.int32)
    return jnp.sum(jnp.where(index[:, None] == spread[None, :], jnp.asarray(table)[None, :], 0), axis=1)


def relative(tile, y, z):
    device = tile >> 2
    dy = ((device >> 2) - y) & 3
    dz = ((device & 3) - z) & 3
    return (dy * SIDE + dz) * 4 + (tile & 3)


def work_list(source, target):
    count = source.shape[0]
    order = jnp.arange(count, dtype=jnp.int32)
    ids = jnp.arange(TILES, dtype=jnp.int32)
    same = target[:, None] == ids[None, :]
    held = jnp.sum(same, axis=0, dtype=jnp.int32)
    before = jnp.sum((target[None, :] == target[:, None]) & (order[None, :] < order[:, None]), axis=1, dtype=jnp.int32)
    entries = jnp.maximum((held + 1) // 2, 1)
    start = jnp.sum(jnp.where(ids[None, :] < ids[:, None], entries[None, :], 0), axis=1)
    mine = jnp.sum(jnp.where(same, start[None, :], 0), axis=1)
    slot = (mine + before // 2) * 2 + before % 2
    value = source + (order << 6) + (1 << 15)
    slots = jnp.arange(2 * ENTRIES, dtype=jnp.int32)
    tiles = jnp.sum(jnp.where(slot[:, None] == slots[None, :], value[:, None], 0), axis=0)
    at = jnp.arange(ENTRIES, dtype=jnp.int32)
    owner = jnp.sum(start[None, :] <= at[:, None], axis=1, dtype=jnp.int32) - 1
    fresh = jnp.sum(start[None, :] == at[:, None], axis=1, dtype=jnp.int32)
    bounds = jnp.concatenate([start, jnp.sum(entries)[None]])
    return tiles, owner * 2 + fresh, bounds


def encode(value):
    top = jnp.max(jnp.abs(value), axis=0, keepdims=True)
    power = jnp.floor(jnp.log2(jnp.maximum(top, 2.0**-100))) + 1.0
    whole = jnp.round(value * jnp.exp2(HALF_RANGE - power)).astype(jnp.int32).astype(jnp.int16)
    return whole, jnp.broadcast_to(power, (PAD, TILE)).astype(jnp.int32).astype(jnp.int16)


def put(ref, k, value):
    whole, power = encode(value)
    ref[k, 0:ROWS, :] = whole
    ref[k, ROWS : ROWS + PAD, :] = power


def get(ref, k):
    power = ref[k, ROWS : ROWS + PAD, :].astype(jnp.int32).astype(jnp.float32)[0:1, :]
    return ref[k, 0:ROWS, :].astype(jnp.int32).astype(jnp.float32) * jnp.exp2(power - HALF_RANGE)


def coded(n):
    return jax.ShapeDtypeStruct((n, ROWS + PAD, TILE), jnp.int16)


def plain(n):
    return jax.ShapeDtypeStruct((n, ROWS, TILE), jnp.float32)


def kernel(body, outs, specs, scratch=(), grant=4):
    return pl.pallas_call(
        body,
        out_shape=outs,
        in_specs=specs,
        out_specs=jax.tree.map(lambda _: VMEM_SPEC, outs),
        scratch_shapes=list(scratch),
        compiler_params=pltpu.CompilerParams(vmem_limit_bytes=grant * 1024 * 1024),
    )


def ladder(tiles, owner, bounds, amps, integrals, first, count, send):
    def body(tiles_ref, owner_ref, bounds_ref, amps_ref, ints_ref, *rest):
        sums = rest[-1] if send else rest[0]
        begin = bounds_ref[first]
        end = bounds_ref[first + count]

        def step(i, carry):
            for k in range(UNROLL):
                at = begin + i * UNROLL + k
                inside = at < end
                at = jnp.minimum(at, ENTRIES - 1)
                left = tiles_ref[2 * at]
                right = tiles_ref[2 * at + 1]
                mark = owner_ref[at]
                place = jnp.where(inside, (mark >> 1) - first, count - 1)
                fresh = jnp.logical_and(inside, (mark & 1) == 1)
                keep_left = jnp.where(inside, left >> 15, 0).astype(jnp.float32).astype(jnp.bfloat16)
                keep_right = jnp.where(inside, right >> 15, 0).astype(jnp.float32).astype(jnp.bfloat16)
                weights = jnp.concatenate(
                    [ints_ref[(left >> 6) & 511] * keep_left, ints_ref[(right >> 6) & 511] * keep_right], axis=0
                )
                values = jnp.concatenate([amps_ref[left & 63], amps_ref[right & 63]], axis=1)
                product = jnp.dot(values, weights, preferred_element_type=jnp.float32)
                sums[place] = product + jnp.where(fresh, 0.0, sums[place])
            return carry

        lax.fori_loop(0, (end - begin + UNROLL - 1) // UNROLL, step, 0)
        if send:
            half = count // 2

            def code(k, carry):
                put(rest[0], k, sums[k])
                put(rest[1], k, sums[k + half])
                return carry

            lax.fori_loop(0, half, code, 0)

    outs = (coded(count // 2), coded(count // 2)) if send else (plain(count),)
    scratch = [pltpu.VMEM((count, ROWS, TILE), jnp.float32)] if send else []
    specs = [SMEM_SPEC] * 3 + [VMEM_SPEC] * 2
    return kernel(body, outs, specs, scratch, 8)(tiles, owner, bounds, amps, integrals)


def masked_tiles(t2, t2_live):
    def body(live_ref, t2_ref, out_ref):
        for t in range(4):
            keep = live_ref[0, t].astype(jnp.float32).astype(jnp.bfloat16)
            out_ref[t] = t2_ref[:, t * TILE : (t + 1) * TILE] * keep

    out = jax.ShapeDtypeStruct((4, ROWS, TILE), jnp.bfloat16)
    return kernel(body, out, [SMEM_SPEC, VMEM_SPEC])(t2_live, t2)


def join(*groups):
    sizes = [[piece.shape[0] for piece in group] for group in groups]

    def body(*refs):
        pieces = refs[: -len(groups)]
        for g, out_ref in enumerate(refs[-len(groups) :]):
            at = 0
            for size in sizes[g]:
                for k in range(size):
                    out_ref[at + k] = pieces[0][k]
                pieces = pieces[1:]
                at += size

    outs = tuple(jax.ShapeDtypeStruct((sum(size), ROWS, TILE), jnp.bfloat16) for size in sizes)
    flat = [piece for group in groups for piece in group]
    return kernel(body, outs, [VMEM_SPEC] * len(flat))(*flat)


def cycle_part(blocks, weights, tiles, base=None):
    def body(blocks_ref, weights_ref, tiles_ref, *rest):
        out_ref = rest[-1]
        for half in range(2):
            cols = slice(half * 2 * TILE, (half + 1) * 2 * TILE)
            total = None if base is None else rest[0][:, cols]
            for k in range(4):
                at = pl.multiple_of(blocks_ref[k] * ROWS, ROWS)
                value = jnp.concatenate([tiles_ref[4 * k + 2 * half], tiles_ref[4 * k + 2 * half + 1]], axis=1)
                part = jnp.dot(weights_ref[:, pl.ds(at, ROWS)], value, preferred_element_type=jnp.float32)
                total = part if total is None else total + part
            out_ref[:, cols] = total

    out = jax.ShapeDtypeStruct((ROWS, 4 * TILE), jnp.float32)
    args = (blocks, weights, tiles) if base is None else (blocks, weights, tiles, base)
    return kernel(body, out, [SMEM_SPEC] + [VMEM_SPEC] * (len(args) - 1))(*args)


def merge(sums, got_up, got_down, base):
    def body(sums_ref, up_ref, down_ref, up_out, down_out):
        def step(k, carry):
            put(up_out, k, sums_ref[base + k] + get(up_ref, k))
            put(down_out, k, sums_ref[base + 4 + k] + get(down_ref, k))
            return carry

        lax.fori_loop(0, 4, step, 0)

    return kernel(body, (coded(4), coded(4)), [VMEM_SPEC] * 3)(sums, got_up, got_down)


def row_sum(sums, got_up, got_down, last_up, last_down, base):
    def body(sums_ref, up_ref, down_ref, last_up_ref, last_down_ref, up_out, down_out, kept):
        def low(k):
            return sums_ref[base + 8 + k] + get(down_ref, 4 + k) + get(last_up_ref, k)

        def high(k):
            return sums_ref[base + 12 + k] + get(up_ref, 4 + k) + get(last_down_ref, k)

        put(up_out, 0, low(2))
        put(up_out, 1, high(1))
        put(down_out, 0, high(2))
        put(down_out, 1, low(3))
        kept[0] = low(1)
        kept[1] = high(3)
        kept[2] = low(0)
        kept[3] = high(0)

    return kernel(body, (coded(2), coded(2), plain(4)), [VMEM_SPEC] * 5)(sums, got_up, got_down, last_up, last_down)


def merge_last(kept, got_up, got_down):
    def body(kept_ref, up_ref, down_ref, up_out, down_out):
        put(up_out, 0, kept_ref[0] + get(up_ref, 0))
        put(down_out, 0, kept_ref[1] + get(down_ref, 0))

    return kernel(body, (coded(1), coded(1)), [VMEM_SPEC] * 3)(kept, got_up, got_down)


def finish(res_live, cycle, half_a, half_b):
    def body(live_ref, cycle_ref, *refs):
        out_ref = refs[-1]
        for h in range(2):
            kept, up, down, last_up, last_down = refs[5 * h : 5 * h + 5]
            low = kept[2] + get(down, 1) + get(last_up, 0)
            high = kept[3] + get(up, 1) + get(last_down, 0)
            for t, value in ((2 * h, low), (2 * h + 1, high)):
                cols = slice(t * TILE, (t + 1) * TILE)
                keep = live_ref[0, t].astype(jnp.float32)
                out_ref[:, cols] = keep * (value + cycle_ref[:, cols])

    out = jax.ShapeDtypeStruct((ROWS, 4 * TILE), jnp.float32)
    return kernel(body, out, [SMEM_SPEC] + [VMEM_SPEC] * 11)(res_live, cycle, *half_a, *half_b)


def local(t2, t2_live, int_tiles, integrals, cycle_w, res_live):
    place = lax.axis_index("ints").astype(jnp.int32)
    y, z = place >> 2, place & 3

    def take(value, dy, dz):
        pairs = [
            (((i + dy) % SIDE) * SIDE + (k + dz) % SIDE, i * SIDE + k) for i in range(SIDE) for k in range(SIDE)
        ]
        return lax.ppermute(value, "ints", pairs)

    def along_z(value, d):
        return take(value, 0, d)

    def along_y(value, d):
        return take(value, d, 0)

    own = masked_tiles(t2, t2_live)
    pair = lax.axis_index("pair").astype(jnp.int32)

    def along_x(value, d, core=0):
        pairs = [(((i + d) % SIDE) * 2 + (c ^ core), i * 2 + c) for i in range(SIDE) for c in range(2)]
        return lax.ppermute(value, "pair", pairs)

    def blocks(core):
        ahead = (pair >> 1) + jnp.array([0, 1, 3, 2], jnp.int32)
        return ((ahead & 3) << 1) | ((pair & 1) ^ core)

    def both(value, axis):
        return axis(value, 1), axis(value, 3)

    def far(value, axis):
        up, down = value
        n = up.shape[0] // 2
        return axis(up[:n], 1), axis(down[n:], 3)

    source = pick(source_table(), relative(int_tiles[:, 0], y, z))
    target = pick(target_table(), relative(int_tiles[:, 1], y, z))
    work = work_list(source, target)

    low, high = own[:2], own[2:]
    near_x = both(own, along_x)
    near_low, near_high, work = lax.optimization_barrier((both(low, along_z), both(high, along_y), work))
    over_low, over_high, near_x = lax.optimization_barrier((far(near_low, along_z), far(near_high, along_y), near_x))
    low, high = join((low, *near_low, *over_low), (high, *near_high, *over_high))
    near_low, near_high, over_x = lax.optimization_barrier(
        (both(low, along_y), both(high, along_z), far(near_x, along_x))
    )
    over_low, over_high = far(near_low, along_y), far(near_high, along_z)
    (mine,) = join((own, *near_x, *over_x))
    other = along_x(mine, 0, 1)
    cycle = cycle_part(blocks(0), cycle_w, mine)
    (amps,) = join((low, *near_low, *over_low, high, *near_high, *over_high))
    amps, cycle = lax.optimization_barrier((amps, cycle))
    cycle = cycle_part(blocks(1), cycle_w, other, cycle)

    send_a = ladder(*work, amps, integrals, 0, 16, True)
    send_b = ladder(*work, amps, integrals, 16, 16, True)

    def first_hop(send, axis):
        return axis(send[0], 3), axis(send[1], 1)

    got_a = first_hop(send_a, along_z)
    got_b = first_hop(send_b, along_y)
    (sums,) = ladder(*work, amps, integrals, 32, 32, False)

    def reduce(got, axis, other, base):
        on = merge(sums, *got, base)
        last = first_hop(on, axis)
        up, down, kept = row_sum(sums, *got, *last, base)
        got = first_hop((up, down), other)
        last = first_hop(merge_last(kept, *got), other)
        return (kept, *got, *last)

    half_a = reduce(got_a, along_z, along_y, 0)
    half_b = reduce(got_b, along_y, along_z, 16)
    return finish(res_live, cycle, half_a, half_b)


def solution(mesh):
    placed = (
        P("pair", "ints"),
        P("pair", "ints"),
        P("ints", None),
        P("ints", None, None),
        P("pair", None),
        P("pair", "ints"),
    )
    return jax.shard_map(local, mesh=mesh, in_specs=placed, out_specs=P("pair", "ints"), check_vma=False)
```

```python
import jax
import jax.numpy as jnp
import numpy as np
from jax import lax
from jax.experimental import pallas as pl
from jax.experimental.pallas import tpu as pltpu
from jax.sharding import PartitionSpec as P

ROWS = 512
TILE = 128
TILES = 64
EARLY = 48
SIDE = 4
PAD = 16
ENTRIES = 224
UNROLL = 8
CODE_UNROLL = 2
HALF_RANGE = 14.9
NEAR = {0: 0, 1: 1, 3: 2, 2: 3}

VMEM_SPEC = pl.BlockSpec(memory_space=pltpu.VMEM)
SMEM_SPEC = pl.BlockSpec(memory_space=pltpu.SMEM)


def source_table():
    table = np.zeros((SIDE, SIDE, 4), np.int32)
    for dy in range(SIDE):
        for dz in range(SIDE):
            for t in range(2):
                for half, (first, second, tile) in enumerate(((dz, dy, t), (dy, dz, t + 2))):
                    row = EARLY + 8 * half if second == 2 else 24 * half + NEAR[second] * 8
                    table[dy, dz, tile] = row + NEAR[first] * 2 + t
    return table.reshape(-1)


def target_table():
    table = np.zeros((SIDE, SIDE, 4), np.int32)
    for far in range(SIDE):
        for other in range(SIDE):
            for t in range(2):
                if far == 2:
                    place = 0 if t == 0 else 8
                elif far == 1:
                    place = 32 if t == 0 else 4
                elif far == 3:
                    place = 12 if t == 0 else 36
                else:
                    place = 40 if t == 0 else 44
                sent = place < 16
                table[other, far, t] = place + other
                table[far, other, t + 2] = place + other + 16
    return table.reshape(-1)


def pick(table, index):
    spread = jnp.arange(TILES, dtype=jnp.int32)
    return jnp.sum(jnp.where(index[:, None] == spread[None, :], jnp.asarray(table)[None, :], 0), axis=1)


def relative(tile, y, z):
    device = tile >> 2
    dy = ((device >> 2) - y) & 3
    dz = ((device & 3) - z) & 3
    return (dy * SIDE + dz) * 4 + (tile & 3)


def work_list(source, target, late):
    member = (source >= EARLY) == late
    count = source.shape[0]
    order = jnp.arange(count, dtype=jnp.int32)
    ids = jnp.arange(TILES, dtype=jnp.int32)
    same = (target[:, None] == ids[None, :]) & member[:, None]
    held = jnp.sum(same, axis=0, dtype=jnp.int32)
    before = jnp.sum((target[None, :] == target[:, None]) & (order[None, :] < order[:, None]) & member[None, :], axis=1, dtype=jnp.int32)
    entries = jnp.maximum((held + 1) // 2, 1)
    start = jnp.sum(jnp.where(ids[None, :] < ids[:, None], entries[None, :], 0), axis=1)
    mine = jnp.sum(jnp.where(same, start[None, :], 0), axis=1)
    slot = jnp.where(member, (mine + before // 2) * 2 + before % 2, -1)
    value = source - EARLY * late + (order << 6) + (1 << 15)
    slots = jnp.arange(2 * ENTRIES, dtype=jnp.int32)
    tiles = jnp.sum(jnp.where(slot[:, None] == slots[None, :], value[:, None], 0), axis=0)
    at = jnp.arange(ENTRIES, dtype=jnp.int32)
    owner = jnp.sum(start[None, :] <= at[:, None], axis=1, dtype=jnp.int32) - 1
    fresh = (at == jnp.sum(jnp.where(owner[:, None] == ids[None, :], start[None, :], 0), axis=1)).astype(jnp.int32)
    bounds = jnp.concatenate([start, jnp.sum(entries)[None]])
    return tiles, owner * 2 + fresh, bounds


def encode(value):
    top = jnp.max(jnp.abs(value), axis=0, keepdims=True)
    power = jnp.floor(jnp.log2(jnp.maximum(top, 2.0**-100))) + 1.0
    whole = jnp.round(value * jnp.exp2(HALF_RANGE - power)).astype(jnp.int32).astype(jnp.int16)
    return whole, jnp.broadcast_to(power, (PAD, TILE)).astype(jnp.int32).astype(jnp.int16)


def put(ref, k, value):
    whole, power = encode(value)
    ref[k, 0:ROWS, :] = whole
    ref[k, ROWS : ROWS + PAD, :] = power


def get(ref, k):
    power = ref[k, ROWS : ROWS + PAD, :].astype(jnp.int32).astype(jnp.float32)[0:1, :]
    return ref[k, 0:ROWS, :].astype(jnp.int32).astype(jnp.float32) * jnp.exp2(power - HALF_RANGE)


def coded(n):
    return jax.ShapeDtypeStruct((n, ROWS + PAD, TILE), jnp.int16)


def plain(n):
    return jax.ShapeDtypeStruct((n, ROWS, TILE), jnp.float32)


def kernel(body, outs, specs, scratch=(), grant=3):
    return pl.pallas_call(
        body,
        out_shape=outs,
        in_specs=specs,
        out_specs=jax.tree.map(lambda _: VMEM_SPEC, outs),
        scratch_shapes=list(scratch),
        compiler_params=pltpu.CompilerParams(vmem_limit_bytes=grant * 1024 * 1024),
    )


def ladder(parts, integrals, first, count, so_far=None):
    def body(*refs):
        ints_ref = refs[4 * len(parts)]
        rest = refs[4 * len(parts) + 1 :]
        sums = rest[-1]
        for p in range(len(parts)):
            tiles_ref, owner_ref, bounds_ref, amps_ref = refs[4 * p : 4 * p + 4]
            begin = bounds_ref[first]
            end = bounds_ref[first + count]
            starts = p == 0

            def step(i, carry):
                for k in range(UNROLL):
                    at = begin + i * UNROLL + k
                    inside = at < end
                    at = jnp.minimum(at, ENTRIES - 1)
                    left = tiles_ref[2 * at]
                    right = tiles_ref[2 * at + 1]
                    mark = owner_ref[at]
                    place = jnp.where(inside, (mark >> 1) - first, count - 1)
                    keep_left = jnp.where(inside, left >> 15, 0).astype(jnp.float32).astype(jnp.bfloat16)
                    keep_right = jnp.where(inside, right >> 15, 0).astype(jnp.float32).astype(jnp.bfloat16)
                    weights = jnp.concatenate(
                        [ints_ref[(left >> 6) & 511] * keep_left, ints_ref[(right >> 6) & 511] * keep_right], axis=0
                    )
                    values = jnp.concatenate([amps_ref[left & 63], amps_ref[right & 63]], axis=1)
                    product = jnp.dot(values, weights, preferred_element_type=jnp.float32)
                    before = sums[place]
                    if starts:
                        before = jnp.where(jnp.logical_and(inside, (mark & 1) == 1), 0.0, before)
                    sums[place] = product + before
                return carry

            lax.fori_loop(0, (end - begin + UNROLL - 1) // UNROLL, step, 0)
        if so_far is not None:
            half = count // 2

            def code(k, carry):
                put(rest[1], k, sums[k] + rest[0][k])
                put(rest[2], k, sums[k + half] + rest[0][k + half])
                return carry

            lax.fori_loop(0, half, code, 0, unroll=CODE_UNROLL)

    args = [value for work, amps in parts for value in (*work, amps)] + [integrals]
    specs = ([SMEM_SPEC] * 3 + [VMEM_SPEC]) * len(parts) + [VMEM_SPEC]
    if so_far is None:
        return kernel(body, plain(count), specs)(*args)
    sums = pltpu.VMEM((count, ROWS, TILE), jnp.float32)
    return kernel(body, (coded(count // 2),) * 2, specs + [VMEM_SPEC], (sums,), 7)(*args, so_far)


def masked_tiles(t2, t2_live):
    def body(live_ref, t2_ref, out_ref):
        for t in range(4):
            keep = live_ref[0, t].astype(jnp.float32).astype(jnp.bfloat16)
            out_ref[t] = t2_ref[:, t * TILE : (t + 1) * TILE] * keep

    out = jax.ShapeDtypeStruct((4, ROWS, TILE), jnp.bfloat16)
    return kernel(body, out, [SMEM_SPEC, VMEM_SPEC])(t2_live, t2)


def join(*groups):
    sizes = [[piece.shape[0] for piece in group] for group in groups]

    def body(*refs):
        pieces = refs[: -len(groups)]
        for g, out_ref in enumerate(refs[-len(groups) :]):
            at = 0
            for size in sizes[g]:
                for k in range(size):
                    out_ref[at + k] = pieces[0][k]
                pieces = pieces[1:]
                at += size

    outs = tuple(jax.ShapeDtypeStruct((sum(size), ROWS, TILE), jnp.bfloat16) for size in sizes)
    flat = [piece for group in groups for piece in group]
    return kernel(body, outs, [VMEM_SPEC] * len(flat))(*flat)


def cycle_part(blocks, weights, tiles, base=None):
    def body(blocks_ref, weights_ref, tiles_ref, *rest):
        out_ref = rest[-1]
        for half in range(2):
            cols = slice(half * 2 * TILE, (half + 1) * 2 * TILE)
            total = None if base is None else rest[0][:, cols]
            for k in range(4):
                at = pl.multiple_of(blocks_ref[k] * ROWS, ROWS)
                value = jnp.concatenate([tiles_ref[4 * k + 2 * half], tiles_ref[4 * k + 2 * half + 1]], axis=1)
                part = jnp.dot(weights_ref[:, pl.ds(at, ROWS)], value, preferred_element_type=jnp.float32)
                total = part if total is None else total + part
            out_ref[:, cols] = total

    out = jax.ShapeDtypeStruct((ROWS, 4 * TILE), jnp.float32)
    args = (blocks, weights, tiles) if base is None else (blocks, weights, tiles, base)
    return kernel(body, out, [SMEM_SPEC] + [VMEM_SPEC] * (len(args) - 1))(*args)


def merge(sums, got_up, got_down):
    def body(sums_ref, up_ref, down_ref, up_out, down_out):
        def step(k, carry):
            put(up_out, k, sums_ref[k] + get(up_ref, k))
            put(down_out, k, sums_ref[4 + k] + get(down_ref, k))
            return carry

        lax.fori_loop(0, 4, step, 0, unroll=CODE_UNROLL)

    return kernel(body, (coded(4), coded(4)), [VMEM_SPEC] * 3)(sums, got_up, got_down)


def row_sum(sums, got_up, got_down, last_up, last_down):
    def body(sums_ref, up_ref, down_ref, last_up_ref, last_down_ref, up_out, down_out, kept):
        def low(k):
            return sums_ref[8 + k] + get(down_ref, 4 + k) + get(last_up_ref, k)

        def high(k):
            return sums_ref[12 + k] + get(up_ref, 4 + k) + get(last_down_ref, k)

        put(up_out, 0, low(2))
        put(up_out, 1, high(1))
        put(down_out, 0, high(2))
        put(down_out, 1, low(3))
        kept[0] = low(1)
        kept[1] = high(3)
        kept[2] = low(0)
        kept[3] = high(0)

    return kernel(body, (coded(2), coded(2), plain(4)), [VMEM_SPEC] * 5)(sums, got_up, got_down, last_up, last_down)


def merge_last(kept, got_up, got_down):
    def body(kept_ref, up_ref, down_ref, up_out, down_out):
        put(up_out, 0, kept_ref[0] + get(up_ref, 0))
        put(down_out, 0, kept_ref[1] + get(down_ref, 0))

    return kernel(body, (coded(1), coded(1)), [VMEM_SPEC] * 3)(kept, got_up, got_down)


def finish(res_live, cycle, half_a, half_b):
    def body(live_ref, cycle_ref, *refs):
        out_ref = refs[-1]
        for h in range(2):
            kept, up, down, last_up, last_down = refs[5 * h : 5 * h + 5]
            low = kept[2] + get(down, 1) + get(last_up, 0)
            high = kept[3] + get(up, 1) + get(last_down, 0)
            for t, value in ((2 * h, low), (2 * h + 1, high)):
                cols = slice(t * TILE, (t + 1) * TILE)
                keep = live_ref[0, t].astype(jnp.float32)
                out_ref[:, cols] = keep * (value + cycle_ref[:, cols])

    out = jax.ShapeDtypeStruct((ROWS, 4 * TILE), jnp.float32)
    return kernel(body, out, [SMEM_SPEC] + [VMEM_SPEC] * 11)(res_live, cycle, *half_a, *half_b)


def local(t2, t2_live, int_tiles, integrals, cycle_w, res_live):
    place = lax.axis_index("ints").astype(jnp.int32)
    y, z = place >> 2, place & 3

    def take(value, dy, dz):
        pairs = [
            (((i + dy) % SIDE) * SIDE + (k + dz) % SIDE, i * SIDE + k) for i in range(SIDE) for k in range(SIDE)
        ]
        return lax.ppermute(value, "ints", pairs)

    def along_z(value, d):
        return take(value, 0, d)

    def along_y(value, d):
        return take(value, d, 0)

    own = masked_tiles(t2, t2_live)
    pair = lax.axis_index("pair").astype(jnp.int32)

    def along_x(value, d, core=0):
        pairs = [(((i + d) % SIDE) * 2 + (c ^ core), i * 2 + c) for i in range(SIDE) for c in range(2)]
        return lax.ppermute(value, "pair", pairs)

    def blocks(core):
        ahead = (pair >> 1) + jnp.array([0, 1, 3, 2], jnp.int32)
        return ((ahead & 3) << 1) | ((pair & 1) ^ core)

    def both(value, axis):
        return axis(value, 1), axis(value, 3)

    def far(value, axis):
        up, down = value
        n = up.shape[0] // 2
        return axis(up[:n], 1), axis(down[n:], 3)

    source = pick(source_table(), relative(int_tiles[:, 0], y, z))
    target = pick(target_table(), relative(int_tiles[:, 1], y, z))

    low, high = own[:2], own[2:]
    near_x = both(own, along_x)
    near_low, near_high, work_1, blocks_1, blocks_2 = lax.optimization_barrier(
        (both(low, along_z), both(high, along_y), work_list(source, target, False), blocks(0), blocks(1))
    )
    low_1, high_1 = join((low, near_low[0]), (high, near_high[0]))
    near_low_1, near_high_1 = both(low_1, along_y), both(high_1, along_z)
    over_low, over_high, near_x, work_2 = lax.optimization_barrier(
        (far(near_low, along_z), far(near_high, along_y), near_x, work_list(source, target, True))
    )
    low_2, high_2 = join((near_low[1], *over_low), (near_high[1], *over_high))
    near_low_2, near_high_2 = both(low_2, along_y), both(high_2, along_z)
    near_low_1, near_high_1, over_x = lax.optimization_barrier((near_low_1, near_high_1, far(near_x, along_x)))
    far_low_1, far_high_1 = along_y(near_low_1[0], 1), along_z(near_high_1[0], 1)
    near_low_2, near_high_2 = lax.optimization_barrier((near_low_2, near_high_2))
    far_low_2, far_high_2 = along_y(near_low_2[1], 3), along_z(near_high_2[1], 3)


    (mine,) = join((own, *near_x, *over_x))
    other = along_x(mine, 0, 1)
    (amps,) = join(
        (low_1, low_2, near_low_1[0], near_low_2[0], near_low_1[1], near_low_2[1])
        + (high_1, high_2, near_high_1[0], near_high_2[0], near_high_1[1], near_high_2[1])
    )
    sums_a = ladder([(work_1, amps)], integrals, 0, 16)
    sums_b = ladder([(work_1, amps)], integrals, 16, 16)
    sums_a, sums_b, *arrived = lax.optimization_barrier(
        (sums_a, sums_b, far_low_1, far_low_2, far_high_1, far_high_2)
    )
    (rest,) = join(arrived)
    send_a = ladder([(work_2, rest)], integrals, 0, 16, sums_a)
    send_b = ladder([(work_2, rest)], integrals, 16, 16, sums_b)

    def first_hop(send, axis):
        return axis(send[0], 3), axis(send[1], 1)

    got_a = first_hop(send_a, along_z)
    got_b = first_hop(send_b, along_y)
    parts = [(work_1, amps), (work_2, rest)]
    sums_a = ladder(parts, integrals, 32, 16)
    sums_b = ladder(parts, integrals, 48, 16)
    cycle = cycle_part(blocks_2, cycle_w, other, cycle_part(blocks_1, cycle_w, mine))
    got_b, cycle = lax.optimization_barrier((got_b, cycle))

    def reduce(sums, got, axis, other):
        on = merge(sums, *got)
        last = first_hop(on, axis)
        up, down, kept = row_sum(sums, *got, *last)
        got = first_hop((up, down), other)
        last = first_hop(merge_last(kept, *got), other)
        return (kept, *got, *last)

    half_a = reduce(sums_a, got_a, along_z, along_y)
    half_b = reduce(sums_b, got_b, along_y, along_z)
    return finish(res_live, cycle, half_a, half_b)


def solution(mesh):
    placed = (
        P("pair", "ints"),
        P("pair", "ints"),
        P("ints", None),
        P("ints", None, None),
        P("pair", None),
        P("pair", "ints"),
    )
    return jax.shard_map(local, mesh=mesh, in_specs=placed, out_specs=P("pair", "ints"), check_vma=False)
```

```python
import jax
import jax.numpy as jnp
import numpy as np
from jax import lax
from jax.experimental import pallas as pl
from jax.experimental.pallas import tpu as pltpu
from jax.sharding import PartitionSpec as P

ROWS = 512
TILE = 128
TILES = 64
EARLY = 48
SIDE = 4
PAD = 16
ENTRIES = 224
UNROLL = 8
CODE_UNROLL = 2
HALF_RANGE = 14.9
NEAR = {0: 0, 1: 1, 3: 2, 2: 3}

VMEM_SPEC = pl.BlockSpec(memory_space=pltpu.VMEM)
SMEM_SPEC = pl.BlockSpec(memory_space=pltpu.SMEM)


def source_table():
    table = np.zeros((SIDE, SIDE, 4), np.int32)
    for dy in range(SIDE):
        for dz in range(SIDE):
            for t in range(2):
                for half, (first, second, tile) in enumerate(((dz, dy, t), (dy, dz, t + 2))):
                    row = EARLY + 8 * half if second == 2 else 24 * half + NEAR[second] * 8
                    table[dy, dz, tile] = row + NEAR[first] * 2 + t
    return table.reshape(-1)


def target_table():
    table = np.zeros((SIDE, SIDE, 4), np.int32)
    for far in range(SIDE):
        for other in range(SIDE):
            for t in range(2):
                if far == 2:
                    place = 0 if t == 0 else 8
                elif far == 1:
                    place = 32 if t == 0 else 4
                elif far == 3:
                    place = 12 if t == 0 else 36
                else:
                    place = 40 if t == 0 else 44
                sent = place < 16
                table[other, far, t] = place + other
                table[far, other, t + 2] = place + other + 16
    return table.reshape(-1)


def pick(table, index):
    spread = jnp.arange(TILES, dtype=jnp.int32)
    return jnp.sum(jnp.where(index[:, None] == spread[None, :], jnp.asarray(table)[None, :], 0), axis=1)


def relative(tile, y, z):
    device = tile >> 2
    dy = ((device >> 2) - y) & 3
    dz = ((device & 3) - z) & 3
    return (dy * SIDE + dz) * 4 + (tile & 3)


def work_list(source, target, late):
    member = (source >= EARLY) == late
    count = source.shape[0]
    order = jnp.arange(count, dtype=jnp.int32)
    ids = jnp.arange(TILES, dtype=jnp.int32)
    same = (target[:, None] == ids[None, :]) & member[:, None]
    held = jnp.sum(same, axis=0, dtype=jnp.int32)
    before = jnp.sum((target[None, :] == target[:, None]) & (order[None, :] < order[:, None]) & member[None, :], axis=1, dtype=jnp.int32)
    entries = jnp.maximum((held + 1) // 2, 1)
    start = jnp.sum(jnp.where(ids[None, :] < ids[:, None], entries[None, :], 0), axis=1)
    mine = jnp.sum(jnp.where(same, start[None, :], 0), axis=1)
    slot = jnp.where(member, (mine + before // 2) * 2 + before % 2, -1)
    value = source - EARLY * late + (order << 6) + (1 << 15)
    slots = jnp.arange(2 * ENTRIES, dtype=jnp.int32)
    tiles = jnp.sum(jnp.where(slot[:, None] == slots[None, :], value[:, None], 0), axis=0)
    at = jnp.arange(ENTRIES, dtype=jnp.int32)
    owner = jnp.sum(start[None, :] <= at[:, None], axis=1, dtype=jnp.int32) - 1
    fresh = (at == jnp.sum(jnp.where(owner[:, None] == ids[None, :], start[None, :], 0), axis=1)).astype(jnp.int32)
    bounds = jnp.concatenate([start, jnp.sum(entries)[None]])
    return tiles, owner * 2 + fresh, bounds


def encode(value):
    top = jnp.max(jnp.abs(value), axis=0, keepdims=True)
    power = jnp.floor(jnp.log2(jnp.maximum(top, 2.0**-100))) + 1.0
    whole = jnp.round(value * jnp.exp2(HALF_RANGE - power)).astype(jnp.int32).astype(jnp.int16)
    return whole, jnp.broadcast_to(power, (PAD, TILE)).astype(jnp.int32).astype(jnp.int16)


def put(ref, k, value):
    whole, power = encode(value)
    ref[k, 0:ROWS, :] = whole
    ref[k, ROWS : ROWS + PAD, :] = power


def get(ref, k):
    power = ref[k, ROWS : ROWS + PAD, :].astype(jnp.int32).astype(jnp.float32)[0:1, :]
    return ref[k, 0:ROWS, :].astype(jnp.int32).astype(jnp.float32) * jnp.exp2(power - HALF_RANGE)


def coded(n):
    return jax.ShapeDtypeStruct((n, ROWS + PAD, TILE), jnp.int16)


def plain(n):
    return jax.ShapeDtypeStruct((n, ROWS, TILE), jnp.float32)


def kernel(body, outs, specs, scratch=(), grant=3):
    return pl.pallas_call(
        body,
        out_shape=outs,
        in_specs=specs,
        out_specs=jax.tree.map(lambda _: VMEM_SPEC, outs),
        scratch_shapes=list(scratch),
        compiler_params=pltpu.CompilerParams(vmem_limit_bytes=grant * 1024 * 1024),
    )


def ladder(parts, integrals, first, count, so_far=None):
    def body(*refs):
        ints_ref = refs[4 * len(parts)]
        rest = refs[4 * len(parts) + 1 :]
        sums = rest[-1]
        for p in range(len(parts)):
            tiles_ref, owner_ref, bounds_ref, amps_ref = refs[4 * p : 4 * p + 4]
            begin = bounds_ref[first]
            end = bounds_ref[first + count]
            starts = p == 0

            def step(i, carry):
                for k in range(UNROLL):
                    at = begin + i * UNROLL + k
                    inside = at < end
                    at = jnp.minimum(at, ENTRIES - 1)
                    left = tiles_ref[2 * at]
                    right = tiles_ref[2 * at + 1]
                    mark = owner_ref[at]
                    place = jnp.where(inside, (mark >> 1) - first, count - 1)
                    keep_left = jnp.where(inside, left >> 15, 0).astype(jnp.float32).astype(jnp.bfloat16)
                    keep_right = jnp.where(inside, right >> 15, 0).astype(jnp.float32).astype(jnp.bfloat16)
                    weights = jnp.concatenate(
                        [ints_ref[(left >> 6) & 511] * keep_left, ints_ref[(right >> 6) & 511] * keep_right], axis=0
                    )
                    values = jnp.concatenate([amps_ref[left & 63], amps_ref[right & 63]], axis=1)
                    product = jnp.dot(values, weights, preferred_element_type=jnp.float32)
                    before = sums[place]
                    if starts:
                        before = jnp.where(jnp.logical_and(inside, (mark & 1) == 1), 0.0, before)
                    sums[place] = product + before
                return carry

            lax.fori_loop(0, (end - begin + UNROLL - 1) // UNROLL, step, 0)
        if so_far is not None:
            half = count // 2

            def code(k, carry):
                put(rest[1], k, sums[k] + rest[0][k])
                put(rest[2], k, sums[k + half] + rest[0][k + half])
                return carry

            lax.fori_loop(0, half, code, 0, unroll=CODE_UNROLL)

    args = [value for work, amps in parts for value in (*work, amps)] + [integrals]
    specs = ([SMEM_SPEC] * 3 + [VMEM_SPEC]) * len(parts) + [VMEM_SPEC]
    if so_far is None:
        return kernel(body, plain(count), specs)(*args)
    sums = pltpu.VMEM((count, ROWS, TILE), jnp.float32)
    return kernel(body, (coded(count // 2),) * 2, specs + [VMEM_SPEC], (sums,), 7)(*args, so_far)


def masked_tiles(t2, t2_live):
    def body(live_ref, t2_ref, out_ref):
        for t in range(4):
            keep = live_ref[0:1, t : t + 1].astype(jnp.float32).astype(jnp.bfloat16)
            out_ref[t] = t2_ref[:, t * TILE : (t + 1) * TILE] * keep

    out = jax.ShapeDtypeStruct((4, ROWS, TILE), jnp.bfloat16)
    return kernel(body, out, [VMEM_SPEC] * 2)(t2_live, t2)


def join(*groups):
    sizes = [[piece.shape[0] for piece in group] for group in groups]

    def body(*refs):
        pieces = refs[: -len(groups)]
        for g, out_ref in enumerate(refs[-len(groups) :]):
            at = 0
            for size in sizes[g]:
                for k in range(size):
                    out_ref[at + k] = pieces[0][k]
                pieces = pieces[1:]
                at += size

    outs = tuple(jax.ShapeDtypeStruct((sum(size), ROWS, TILE), jnp.bfloat16) for size in sizes)
    flat = [piece for group in groups for piece in group]
    return kernel(body, outs, [VMEM_SPEC] * len(flat))(*flat)


def cycle_part(blocks, weights, tiles, base=None):
    def body(blocks_ref, weights_ref, tiles_ref, *rest):
        out_ref = rest[-1]
        for half in range(2):
            cols = slice(half * 2 * TILE, (half + 1) * 2 * TILE)
            total = None if base is None else rest[0][:, cols]
            for k in range(4):
                at = pl.multiple_of(blocks_ref[k] * ROWS, ROWS)
                value = jnp.concatenate([tiles_ref[4 * k + 2 * half], tiles_ref[4 * k + 2 * half + 1]], axis=1)
                part = jnp.dot(weights_ref[:, pl.ds(at, ROWS)], value, preferred_element_type=jnp.float32)
                total = part if total is None else total + part
            out_ref[:, cols] = total

    out = jax.ShapeDtypeStruct((ROWS, 4 * TILE), jnp.float32)
    args = (blocks, weights, tiles) if base is None else (blocks, weights, tiles, base)
    return kernel(body, out, [SMEM_SPEC] + [VMEM_SPEC] * (len(args) - 1))(*args)


def merge(sums, got_up, got_down):
    def body(sums_ref, up_ref, down_ref, up_out, down_out):
        def step(k, carry):
            put(up_out, k, sums_ref[k] + get(up_ref, k))
            put(down_out, k, sums_ref[4 + k] + get(down_ref, k))
            return carry

        lax.fori_loop(0, 4, step, 0, unroll=CODE_UNROLL)

    return kernel(body, (coded(4), coded(4)), [VMEM_SPEC] * 3)(sums, got_up, got_down)


def row_sum(sums, got_up, got_down, last_up, last_down):
    def body(sums_ref, up_ref, down_ref, last_up_ref, last_down_ref, up_out, down_out, kept):
        def low(k):
            return sums_ref[8 + k] + get(down_ref, 4 + k) + get(last_up_ref, k)

        def high(k):
            return sums_ref[12 + k] + get(up_ref, 4 + k) + get(last_down_ref, k)

        put(up_out, 0, low(2))
        put(up_out, 1, high(1))
        put(down_out, 0, high(2))
        put(down_out, 1, low(3))
        kept[0] = low(1)
        kept[1] = high(3)
        kept[2] = low(0)
        kept[3] = high(0)

    return kernel(body, (coded(2), coded(2), plain(4)), [VMEM_SPEC] * 5)(sums, got_up, got_down, last_up, last_down)


def merge_last(kept, got_up, got_down):
    def body(kept_ref, up_ref, down_ref, up_out, down_out):
        put(up_out, 0, kept_ref[0] + get(up_ref, 0))
        put(down_out, 0, kept_ref[1] + get(down_ref, 0))

    return kernel(body, (coded(1), coded(1)), [VMEM_SPEC] * 3)(kept, got_up, got_down)


def add_direct(kept, got_up, got_down):
    def body(kept_ref, up_ref, down_ref, out_ref):
        out_ref[0] = kept_ref[2] + get(down_ref, 1)
        out_ref[1] = kept_ref[3] + get(up_ref, 1)

    return kernel(body, plain(2), [VMEM_SPEC] * 3)(kept, got_up, got_down)


def finish(res_live, cycle, half_a, half_b):
    def body(live_ref, cycle_ref, *refs):
        out_ref = refs[-1]
        for h in range(2):
            own, last_up, last_down = refs[3 * h : 3 * h + 3]
            for t, last in ((0, last_up), (1, last_down)):
                cols = slice((2 * h + t) * TILE, (2 * h + t + 1) * TILE)
                keep = live_ref[0:1, 2 * h + t : 2 * h + t + 1].astype(jnp.float32)
                out_ref[:, cols] = keep * (own[t] + get(last, 0) + cycle_ref[:, cols])

    out = jax.ShapeDtypeStruct((ROWS, 4 * TILE), jnp.float32)
    return kernel(body, out, [VMEM_SPEC] * 8)(res_live, cycle, *half_a, *half_b)


def local(t2, t2_live, int_tiles, integrals, cycle_w, res_live):
    place = lax.axis_index("ints").astype(jnp.int32)
    y, z = place >> 2, place & 3

    def take(value, dy, dz):
        pairs = [
            (((i + dy) % SIDE) * SIDE + (k + dz) % SIDE, i * SIDE + k) for i in range(SIDE) for k in range(SIDE)
        ]
        return lax.ppermute(value, "ints", pairs)

    def along_z(value, d):
        return take(value, 0, d)

    def along_y(value, d):
        return take(value, d, 0)

    own = masked_tiles(t2, t2_live)
    pair = lax.axis_index("pair").astype(jnp.int32)

    def along_x(value, d, core=0):
        pairs = [(((i + d) % SIDE) * 2 + (c ^ core), i * 2 + c) for i in range(SIDE) for c in range(2)]
        return lax.ppermute(value, "pair", pairs)

    def blocks(core):
        ahead = (pair >> 1) + jnp.array([0, 1, 3, 2], jnp.int32)
        return ((ahead & 3) << 1) | ((pair & 1) ^ core)

    def both(value, axis):
        return axis(value, 1), axis(value, 3)

    def far(value, axis):
        up, down = value
        n = up.shape[0] // 2
        return axis(up[:n], 1), axis(down[n:], 3)

    source = pick(source_table(), relative(int_tiles[:, 0], y, z))
    target = pick(target_table(), relative(int_tiles[:, 1], y, z))

    low, high = own[:2], own[2:]
    near_x = both(own, along_x)
    near_low, near_high, work_1, blocks_1, blocks_2 = lax.optimization_barrier(
        (both(low, along_z), both(high, along_y), work_list(source, target, False), blocks(0), blocks(1))
    )
    low_1, high_1 = join((low, near_low[0]), (high, near_high[0]))
    near_low_1, near_high_1 = both(low_1, along_y), both(high_1, along_z)
    over_low, over_high, near_x, work_2 = lax.optimization_barrier(
        (far(near_low, along_z), far(near_high, along_y), near_x, work_list(source, target, True))
    )
    low_2, high_2 = join((near_low[1], *over_low), (near_high[1], *over_high))
    near_low_2, near_high_2 = both(low_2, along_y), both(high_2, along_z)
    near_low_1, near_high_1, over_x = lax.optimization_barrier((near_low_1, near_high_1, far(near_x, along_x)))
    far_low_1, far_high_1 = along_y(near_low_1[0], 1), along_z(near_high_1[0], 1)
    near_low_2, near_high_2 = lax.optimization_barrier((near_low_2, near_high_2))
    far_low_2, far_high_2 = along_y(near_low_2[1], 3), along_z(near_high_2[1], 3)


    (mine,) = join((own, *near_x, *over_x))
    other = along_x(mine, 0, 1)
    (amps,) = join(
        (low_1, low_2, near_low_1[0], near_low_2[0], near_low_1[1], near_low_2[1])
        + (high_1, high_2, near_high_1[0], near_high_2[0], near_high_1[1], near_high_2[1])
    )
    sums_a = ladder([(work_1, amps)], integrals, 0, 16)
    sums_b = ladder([(work_1, amps)], integrals, 16, 16)
    sums_a, sums_b, *arrived = lax.optimization_barrier(
        (sums_a, sums_b, far_low_1, far_low_2, far_high_1, far_high_2)
    )
    (rest,) = join(arrived)
    send_a = ladder([(work_2, rest)], integrals, 0, 16, sums_a)
    send_b = ladder([(work_2, rest)], integrals, 16, 16, sums_b)

    def first_hop(send, axis):
        return axis(send[0], 3), axis(send[1], 1)

    got_a = first_hop(send_a, along_z)
    got_b = first_hop(send_b, along_y)
    parts = [(work_1, amps), (work_2, rest)]
    sums_a = ladder(parts, integrals, 32, 16)
    sums_b = ladder(parts, integrals, 48, 16)
    cycle = cycle_part(blocks_2, cycle_w, other, cycle_part(blocks_1, cycle_w, mine))
    got_b, cycle = lax.optimization_barrier((got_b, cycle))

    def reduce(sums, got, axis, other):
        on = merge(sums, *got)
        last = first_hop(on, axis)
        up, down, kept = row_sum(sums, *got, *last)
        got = first_hop((up, down), other)
        last = first_hop(merge_last(kept, *got), other)
        return (add_direct(kept, *got), *last)

    half_a = reduce(sums_a, got_a, along_z, along_y)
    half_b = reduce(sums_b, got_b, along_y, along_z)
    return finish(res_live, cycle, half_a, half_b)


def solution(mesh):
    placed = (
        P("pair", "ints"),
        P("pair", "ints"),
        P("ints", None),
        P("ints", None, None),
        P("pair", None),
        P("pair", "ints"),
    )
    return jax.shard_map(local, mesh=mesh, in_specs=placed, out_specs=P("pair", "ints"), check_vma=False)
```

```python
import jax
import jax.numpy as jnp
import numpy as np
from jax import lax
from jax.experimental import pallas as pl
from jax.experimental.pallas import tpu as pltpu
from jax.sharding import PartitionSpec as P

ROWS = 512
TILE = 128
TILES = 64
EARLY = 48
SIDE = 4
PAD = 16
ENTRIES = 224
UNROLL = 8
CODE_UNROLL = 2
HALF_RANGE = 14.9
NEAR = {0: 0, 1: 1, 3: 2, 2: 3}

VMEM_SPEC = pl.BlockSpec(memory_space=pltpu.VMEM)
SMEM_SPEC = pl.BlockSpec(memory_space=pltpu.SMEM)


def source_table():
    table = np.zeros((SIDE, SIDE, 4), np.int32)
    for dy in range(SIDE):
        for dz in range(SIDE):
            for t in range(2):
                for half, (first, second, tile) in enumerate(((dz, dy, t), (dy, dz, t + 2))):
                    row = EARLY + 8 * half if second == 2 else 24 * half + NEAR[second] * 8
                    table[dy, dz, tile] = row + NEAR[first] * 2 + t
    return table.reshape(-1)


def target_table():
    table = np.zeros((SIDE, SIDE, 4), np.int32)
    for far in range(SIDE):
        for other in range(SIDE):
            for t in range(2):
                if far == 2:
                    place = 0 if t == 0 else 8
                elif far == 1:
                    place = 32 if t == 0 else 4
                elif far == 3:
                    place = 12 if t == 0 else 36
                else:
                    place = 40 if t == 0 else 44
                sent = place < 16
                table[other, far, t] = place + other
                table[far, other, t + 2] = place + other + 16
    return table.reshape(-1)


def pick(table, index):
    spread = jnp.arange(TILES, dtype=jnp.int32)
    return jnp.sum(jnp.where(index[:, None] == spread[None, :], jnp.asarray(table)[None, :], 0), axis=1)


def relative(tile, y, z):
    device = tile >> 2
    dy = ((device >> 2) - y) & 3
    dz = ((device & 3) - z) & 3
    return (dy * SIDE + dz) * 4 + (tile & 3)


def work_list(source, target, late):
    member = (source >= EARLY) == late
    count = source.shape[0]
    order = jnp.arange(count, dtype=jnp.int32)
    ids = jnp.arange(TILES, dtype=jnp.int32)
    same = (target[:, None] == ids[None, :]) & member[:, None]
    held = jnp.sum(same, axis=0, dtype=jnp.int32)
    before = jnp.sum((target[None, :] == target[:, None]) & (order[None, :] < order[:, None]) & member[None, :], axis=1, dtype=jnp.int32)
    entries = jnp.maximum((held + 1) // 2, jnp.where(ids < 32, 1, 0) if late else 1)
    start = jnp.sum(jnp.where(ids[None, :] < ids[:, None], entries[None, :], 0), axis=1)
    mine = jnp.sum(jnp.where(same, start[None, :], 0), axis=1)
    slot = jnp.where(member, (mine + before // 2) * 2 + before % 2, -1)
    value = source - EARLY * late + (order << 6) + (1 << 15)
    slots = jnp.arange(2 * ENTRIES, dtype=jnp.int32)
    tiles = jnp.sum(jnp.where(slot[:, None] == slots[None, :], value[:, None], 0), axis=0)
    at = jnp.arange(ENTRIES, dtype=jnp.int32)
    owner = jnp.sum(start[None, :] <= at[:, None], axis=1, dtype=jnp.int32) - 1
    fresh = (at == jnp.sum(jnp.where(owner[:, None] == ids[None, :], start[None, :], 0), axis=1)).astype(jnp.int32)
    bounds = jnp.concatenate([start, jnp.sum(entries)[None]])
    return tiles, owner * 2 + fresh, bounds


def encode(value):
    top = jnp.max(jnp.abs(value), axis=0, keepdims=True)
    power = jnp.floor(jnp.log2(jnp.maximum(top, 2.0**-100))) + 1.0
    whole = jnp.round(value * jnp.exp2(HALF_RANGE - power)).astype(jnp.int32).astype(jnp.int16)
    return whole, jnp.broadcast_to(power, (PAD, TILE)).astype(jnp.int32).astype(jnp.int16)


def put(ref, k, value):
    whole, power = encode(value)
    ref[k, 0:ROWS, :] = whole
    ref[k, ROWS : ROWS + PAD, :] = power


def get(ref, k):
    power = ref[k, ROWS : ROWS + PAD, :].astype(jnp.int32).astype(jnp.float32)[0:1, :]
    return ref[k, 0:ROWS, :].astype(jnp.int32).astype(jnp.float32) * jnp.exp2(power - HALF_RANGE)


def coded(n):
    return jax.ShapeDtypeStruct((n, ROWS + PAD, TILE), jnp.int16)


def plain(n):
    return jax.ShapeDtypeStruct((n, ROWS, TILE), jnp.float32)


def kernel(body, outs, specs, scratch=(), grant=3):
    return pl.pallas_call(
        body,
        out_shape=outs,
        in_specs=specs,
        out_specs=jax.tree.map(lambda _: VMEM_SPEC, outs),
        scratch_shapes=list(scratch),
        compiler_params=pltpu.CompilerParams(vmem_limit_bytes=grant * 1024 * 1024),
    )


def ladder(parts, integrals, first, count, so_far=None):
    def body(*refs):
        ints_ref = refs[4 * len(parts)]
        rest = refs[4 * len(parts) + 1 :]
        sums = rest[-1]
        for p in range(len(parts)):
            tiles_ref, owner_ref, bounds_ref, amps_ref = refs[4 * p : 4 * p + 4]
            begin = bounds_ref[first]
            end = bounds_ref[first + count]
            starts = p == 0

            def step(i, carry):
                for k in range(UNROLL):
                    at = begin + i * UNROLL + k
                    inside = at < end
                    at = jnp.minimum(at, ENTRIES - 1)
                    left = tiles_ref[2 * at]
                    right = tiles_ref[2 * at + 1]
                    mark = owner_ref[at]
                    place = jnp.where(inside, (mark >> 1) - first, count - 1)
                    keep_left = jnp.where(inside, left >> 15, 0).astype(jnp.float32).astype(jnp.bfloat16)
                    keep_right = jnp.where(inside, right >> 15, 0).astype(jnp.float32).astype(jnp.bfloat16)
                    weights = jnp.concatenate(
                        [ints_ref[(left >> 6) & 511] * keep_left, ints_ref[(right >> 6) & 511] * keep_right], axis=0
                    )
                    values = jnp.concatenate([amps_ref[left & 63], amps_ref[right & 63]], axis=1)
                    product = jnp.dot(values, weights, preferred_element_type=jnp.float32)
                    before = sums[place]
                    if starts:
                        before = jnp.where(jnp.logical_and(inside, (mark & 1) == 1), 0.0, before)
                    sums[place] = product + before
                return carry

            lax.fori_loop(0, (end - begin + UNROLL - 1) // UNROLL, step, 0)
        if so_far is not None:
            half = count // 2

            def code(k, carry):
                put(rest[1], k, sums[k] + rest[0][k])
                put(rest[2], k, sums[k + half] + rest[0][k + half])
                return carry

            lax.fori_loop(0, half, code, 0, unroll=CODE_UNROLL)

    args = [value for work, amps in parts for value in (*work, amps)] + [integrals]
    specs = ([SMEM_SPEC] * 3 + [VMEM_SPEC]) * len(parts) + [VMEM_SPEC]
    if so_far is None:
        return kernel(body, plain(count), specs)(*args)
    sums = pltpu.VMEM((count, ROWS, TILE), jnp.float32)
    return kernel(body, (coded(count // 2),) * 2, specs + [VMEM_SPEC], (sums,), 7)(*args, so_far)


def masked_tiles(t2, t2_live):
    def body(live_ref, t2_ref, out_ref):
        for t in range(4):
            keep = live_ref[0:1, t : t + 1].astype(jnp.float32).astype(jnp.bfloat16)
            out_ref[t] = t2_ref[:, t * TILE : (t + 1) * TILE] * keep

    out = jax.ShapeDtypeStruct((4, ROWS, TILE), jnp.bfloat16)
    return kernel(body, out, [VMEM_SPEC] * 2)(t2_live, t2)


def join(*groups):
    sizes = [[piece.shape[0] for piece in group] for group in groups]

    def body(*refs):
        pieces = refs[: -len(groups)]
        for g, out_ref in enumerate(refs[-len(groups) :]):
            at = 0
            for size in sizes[g]:
                for k in range(size):
                    out_ref[at + k] = pieces[0][k]
                pieces = pieces[1:]
                at += size

    outs = tuple(jax.ShapeDtypeStruct((sum(size), ROWS, TILE), jnp.bfloat16) for size in sizes)
    flat = [piece for group in groups for piece in group]
    return kernel(body, outs, [VMEM_SPEC] * len(flat))(*flat)


def cycle_part(blocks, weights, tiles, base=None):
    def body(blocks_ref, weights_ref, tiles_ref, *rest):
        out_ref = rest[-1]
        for half in range(2):
            cols = slice(half * 2 * TILE, (half + 1) * 2 * TILE)
            total = None if base is None else rest[0][:, cols]
            for k in range(4):
                at = pl.multiple_of(blocks_ref[k] * ROWS, ROWS)
                value = jnp.concatenate([tiles_ref[4 * k + 2 * half], tiles_ref[4 * k + 2 * half + 1]], axis=1)
                part = jnp.dot(weights_ref[:, pl.ds(at, ROWS)], value, preferred_element_type=jnp.float32)
                total = part if total is None else total + part
            out_ref[:, cols] = total

    out = jax.ShapeDtypeStruct((ROWS, 4 * TILE), jnp.float32)
    args = (blocks, weights, tiles) if base is None else (blocks, weights, tiles, base)
    return kernel(body, out, [SMEM_SPEC] + [VMEM_SPEC] * (len(args) - 1))(*args)


def merge(sums, got_up, got_down):
    def body(sums_ref, up_ref, down_ref, up_out, down_out):
        def step(k, carry):
            put(up_out, k, sums_ref[k] + get(up_ref, k))
            put(down_out, k, sums_ref[4 + k] + get(down_ref, k))
            return carry

        lax.fori_loop(0, 4, step, 0, unroll=CODE_UNROLL)

    return kernel(body, (coded(4), coded(4)), [VMEM_SPEC] * 3)(sums, got_up, got_down)


def row_sum(sums, got_up, got_down, last_up, last_down):
    def body(sums_ref, up_ref, down_ref, last_up_ref, last_down_ref, up_out, down_out, kept):
        def low(k):
            return sums_ref[8 + k] + get(down_ref, 4 + k) + get(last_up_ref, k)

        def high(k):
            return sums_ref[12 + k] + get(up_ref, 4 + k) + get(last_down_ref, k)

        put(up_out, 0, low(2))
        put(up_out, 1, high(1))
        put(down_out, 0, high(2))
        put(down_out, 1, low(3))
        kept[0] = low(1)
        kept[1] = high(3)
        kept[2] = low(0)
        kept[3] = high(0)

    return kernel(body, (coded(2), coded(2), plain(4)), [VMEM_SPEC] * 5)(sums, got_up, got_down, last_up, last_down)


def merge_last(kept, got_up, got_down):
    def body(kept_ref, up_ref, down_ref, up_out, down_out):
        put(up_out, 0, kept_ref[0] + get(up_ref, 0))
        put(down_out, 0, kept_ref[1] + get(down_ref, 0))

    return kernel(body, (coded(1), coded(1)), [VMEM_SPEC] * 3)(kept, got_up, got_down)


def add_direct(kept, got_up, got_down):
    def body(kept_ref, up_ref, down_ref, out_ref):
        out_ref[0] = kept_ref[2] + get(down_ref, 1)
        out_ref[1] = kept_ref[3] + get(up_ref, 1)

    return kernel(body, plain(2), [VMEM_SPEC] * 3)(kept, got_up, got_down)


def finish(res_live, cycle, half_a, half_b):
    def body(live_ref, cycle_ref, *refs):
        out_ref = refs[-1]
        for h in range(2):
            own, last_up, last_down = refs[3 * h : 3 * h + 3]
            for t, last in ((0, last_up), (1, last_down)):
                cols = slice((2 * h + t) * TILE, (2 * h + t + 1) * TILE)
                keep = live_ref[0:1, 2 * h + t : 2 * h + t + 1].astype(jnp.float32)
                out_ref[:, cols] = keep * (own[t] + get(last, 0) + cycle_ref[:, cols])

    out = jax.ShapeDtypeStruct((ROWS, 4 * TILE), jnp.float32)
    return kernel(body, out, [VMEM_SPEC] * 8)(res_live, cycle, *half_a, *half_b)


def local(t2, t2_live, int_tiles, integrals, cycle_w, res_live):
    place = lax.axis_index("ints").astype(jnp.int32)
    y, z = place >> 2, place & 3

    def take(value, dy, dz):
        pairs = [
            (((i + dy) % SIDE) * SIDE + (k + dz) % SIDE, i * SIDE + k) for i in range(SIDE) for k in range(SIDE)
        ]
        return lax.ppermute(value, "ints", pairs)

    def along_z(value, d):
        return take(value, 0, d)

    def along_y(value, d):
        return take(value, d, 0)

    own = masked_tiles(t2, t2_live)
    pair = lax.axis_index("pair").astype(jnp.int32)

    def along_x(value, d, core=0):
        pairs = [(((i + d) % SIDE) * 2 + (c ^ core), i * 2 + c) for i in range(SIDE) for c in range(2)]
        return lax.ppermute(value, "pair", pairs)

    def blocks(core):
        ahead = (pair >> 1) + jnp.array([0, 1, 3, 2], jnp.int32)
        return ((ahead & 3) << 1) | ((pair & 1) ^ core)

    def both(value, axis):
        return axis(value, 1), axis(value, 3)

    def far(value, axis):
        up, down = value
        n = up.shape[0] // 2
        return axis(up[:n], 1), axis(down[n:], 3)

    source = pick(source_table(), relative(int_tiles[:, 0], y, z))
    target = pick(target_table(), relative(int_tiles[:, 1], y, z))

    low, high = own[:2], own[2:]
    near_x = both(own, along_x)
    near_low, near_high, work_1, blocks_1, blocks_2 = lax.optimization_barrier(
        (both(low, along_z), both(high, along_y), work_list(source, target, False), blocks(0), blocks(1))
    )
    low_1, high_1 = join((low, near_low[0]), (high, near_high[0]))
    near_low_1, near_high_1 = both(low_1, along_y), both(high_1, along_z)
    over_low, over_high, near_x, work_2 = lax.optimization_barrier(
        (far(near_low, along_z), far(near_high, along_y), near_x, work_list(source, target, True))
    )
    low_2, high_2 = join((near_low[1], *over_low), (near_high[1], *over_high))
    near_low_2, near_high_2 = both(low_2, along_y), both(high_2, along_z)
    near_low_1, near_high_1, over_x = lax.optimization_barrier((near_low_1, near_high_1, far(near_x, along_x)))
    far_low_1, far_high_1 = along_y(near_low_1[0], 1), along_z(near_high_1[0], 1)
    near_low_2, near_high_2 = lax.optimization_barrier((near_low_2, near_high_2))
    far_low_2, far_high_2 = along_y(near_low_2[1], 3), along_z(near_high_2[1], 3)


    (mine,) = join((own, *near_x, *over_x))
    other = along_x(mine, 0, 1)
    (amps,) = join(
        (low_1, low_2, near_low_1[0], near_low_2[0], near_low_1[1], near_low_2[1])
        + (high_1, high_2, near_high_1[0], near_high_2[0], near_high_1[1], near_high_2[1])
    )
    sums_a = ladder([(work_1, amps)], integrals, 0, 16)
    sums_b = ladder([(work_1, amps)], integrals, 16, 16)
    sums_a, sums_b, *arrived = lax.optimization_barrier(
        (sums_a, sums_b, far_low_1, far_low_2, far_high_1, far_high_2)
    )
    (rest,) = join(arrived)
    send_a = ladder([(work_2, rest)], integrals, 0, 16, sums_a)
    send_b = ladder([(work_2, rest)], integrals, 16, 16, sums_b)

    def first_hop(send, axis):
        return axis(send[0], 3), axis(send[1], 1)

    got_a = first_hop(send_a, along_z)
    got_b = first_hop(send_b, along_y)
    parts = [(work_1, amps), (work_2, rest)]
    sums_a = ladder(parts, integrals, 32, 16)
    sums_b = ladder(parts, integrals, 48, 16)
    cycle = cycle_part(blocks_2, cycle_w, other, cycle_part(blocks_1, cycle_w, mine))
    got_b, cycle = lax.optimization_barrier((got_b, cycle))

    def reduce(sums, got, axis, other):
        on = merge(sums, *got)
        last = first_hop(on, axis)
        up, down, kept = row_sum(sums, *got, *last)
        got = first_hop((up, down), other)
        last = first_hop(merge_last(kept, *got), other)
        return (add_direct(kept, *got), *last)

    half_a = reduce(sums_a, got_a, along_z, along_y)
    half_b = reduce(sums_b, got_b, along_y, along_z)
    return finish(res_live, cycle, half_a, half_b)


def solution(mesh):
    placed = (
        P("pair", "ints"),
        P("pair", "ints"),
        P("ints", None),
        P("ints", None, None),
        P("pair", None),
        P("pair", "ints"),
    )
    return jax.shard_map(local, mesh=mesh, in_specs=placed, out_specs=P("pair", "ints"), check_vma=False)
```
